32 devices in a mesh: rollout: 4 (over y, core), row: 2 (over x), col: 4 (over z).
Axes of the slice: x: 2, y: 2, z: 4, core: 2. Of those that a mesh axis runs over, the one named last changes fastest.
Arguments:
- queries: bfloat16 [4096, 4096], P(('rollout', 'row', 'col')), may hold values from -16 to 16
- keys: bfloat16 [4096, 512], P(('rollout', 'row', 'col')), may hold values from -16 to 16
- values: bfloat16 [4096, 512], P(('rollout', 'row', 'col')), may hold values from -6 to 6
- out_grad: bfloat16 [4096, 4096], P(('rollout', 'row', 'col')), may hold values from -12 to 12
- hidden_in: bfloat16 [4096, 8192], P(('rollout', 'col'), 'row'), may hold values from -1.5 to 1.5
- q_weight: bfloat16 [4096, 8192], P('col', 'row'), may hold values from -0.09375 to 0.09375
- lengths: int32 [4, 32], P('rollout'), may hold values from 1 to 64, 1024 in all within a row
- kv_order: int32 [4], replicated, may hold values from 0 to 3, each once
Outputs:
- key_grad: float32 [4096, 512], P(('rollout', 'row', 'col'))
- value_grad: float32 [4096, 512], P(('rollout', 'row', 'col'))
- input_grad: bfloat16 [4096, 8192], P(('rollout', 'col'), 'row')
- weight_grad: float32 [4096, 8192], P(('rollout', 'col'), 'row')
The draws below stay inside these ranges and needn't reach their ends.
Inputs may be any that keep to these rules, and one draw needn't show every extreme that they name: `lengths`: each row lists, for 16 packed rollouts in order, a prompt length and then a response length; a row sums to 1024 and its largest entry is exactly 64. `kv_order`: A permutation of the 4 key-value heads.
All inputs are finite; a program needn't handle non-finite values.
Results may differ from the reference program's by a relative error of at most 0.0057.
Values may be sent and summed in bfloat16 or wider, within the bound.
A program may use at most 192 MiB of HBM per device.

```python
import math
import jax
import jax.numpy as jnp
import numpy as np
from jax import lax

D = 8192
HQ = 32
KV = 4
HD = 128
ROLLS = 16
GROUPS = 4
TOK_G = 1024
TOKENS = 4096
MOST = 64
N_ROLLOUT = 4


def paired_draw(key):
    query_key = jax.random.fold_in(key, 101)
    key_key = jax.random.fold_in(key, 202)
    query_vals = jnp.clip(jax.random.normal(query_key, (TOKENS, HQ * HD), jnp.float32), -4.0, 4.0)
    key_vals = jnp.clip(jax.random.normal(key_key, (TOKENS, KV * HD), jnp.float32), -4.0, 4.0)
    return (query_vals, key_vals)


def draw_queries(key, part):
    return paired_draw(key)[0].astype(jnp.bfloat16)


def draw_keys(key, part):
    return paired_draw(key)[1].astype(jnp.bfloat16)


def block_scale(key, extent, shards, smallest, high):
    gain, own = 1.0, jax.random.fold_in(key, 6)
    for dim, blocks in shards:
        draws = jnp.exp(jax.random.uniform(jax.random.fold_in(own, dim), (blocks,), jnp.float32, smallest / len(shards), high / len(shards)))
        gain = gain * jnp.repeat(draws, extent[dim] // blocks).reshape([-1 if axis == dim else 1 for axis in range(len(extent))])
    return gain


def profile(amount, total, most, skew):
    loads = [(1 << 20) // math.isqrt(rank ** skew) + 1 for rank in range(2, amount + 1)]
    spare, holding = total - most - (amount - 1), [1] * (amount - 1)
    while spare > 0:
        free = [i for i in range(amount - 1) if holding[i] < most]
        pool, remaining = sum([loads[i] for i in free]), spare
        for i in free:
            extra = min(most - holding[i], max(1, remaining * loads[i] // pool), spare)
            holding[i] = holding[i] + extra
            spare = spare - extra
    return np.array([most] + holding)


def uneven(key, count, total, bound, skew):
    if count == 2:
        one = jax.random.randint(key, (), max(1, total - bound), min(bound, total - 1) + 1)
        return jnp.stack([one, total - one])
    sizes = jnp.asarray(profile(count, total, bound, skew), jnp.int32)
    couples = (count - 1) // 2
    giver, receiver = sizes[1:1 + 2 * couples:2], sizes[2:2 + 2 * couples:2]
    slack = jnp.minimum(giver - 1, bound - receiver)
    shifted = jax.random.randint(jax.random.fold_in(key, 1), (couples,), 0, 1 << 20) % (slack + 1)
    sizes = sizes.at[1:1 + 2 * couples:2].set(giver - shifted).at[2:2 + 2 * couples:2].set(receiver + shifted)
    return sizes[jax.random.permutation(jax.random.fold_in(key, 2), count)]


def gaussian(key, shape, scale, most, cuts=(), held_as=jnp.bfloat16):
    gain = block_scale(key, shape, cuts, -0.22, 0.18) if cuts else 1.0
    values = jax.random.normal(key, shape, jnp.float32) * scale * gain
    return jnp.minimum(jnp.maximum(values, -most), most).astype(held_as)


def setup_inputs(seed: int = 0) -> dict:
    splits = jax.random.split(jax.random.key(seed), 9)
    return {
        "queries": draw_queries(jax.random.fold_in(splits[8], 71), 0),
        "keys": draw_keys(jax.random.fold_in(splits[8], 71), 0),
        "values": gaussian(splits[2], (TOKENS, KV * HD), 1.0, 6.0, ((0, 32),)),
        "out_grad": gaussian(splits[3], (TOKENS, HQ * HD), 2.0, 12.0, ((0, 32),)),
        "hidden_in": gaussian(splits[4], (TOKENS, D), 0.25, 1.5, ((0, 16), (1, 2))),
        "q_weight": gaussian(splits[5], (HQ * HD, D), (HQ * HD) ** -0.5, 0.09375, ((0, 4), (1, 2))),
        "lengths": jax.vmap(lambda own: uneven(own, 2 * ROLLS, TOK_G, MOST, 1))(jax.random.split(splits[6], GROUPS)).reshape((GROUPS, 2 * ROLLS)).astype(jnp.int32),
        "kv_order": jax.random.permutation(splits[7], KV).astype(jnp.int32),
    }


def token_parts(lengths_row, length_total):
    bounds = jnp.cumsum(lengths_row).astype(jnp.int32)
    position = jnp.arange(length_total, dtype=jnp.int32)
    return lax.optimization_barrier(jnp.sum((position[:, None] >= bounds[None, :]).astype(jnp.int32), axis=1)).astype(jnp.int32)

def group_grads(queries, keys, values, out_grad, lengths_row, kv_order):
    scale_factor = 1.0 / math.sqrt(HD)
    parts = token_parts(lengths_row, TOK_G)
    document = parts // 2
    response = (parts % 2).astype(jnp.bfloat16)
    position = jnp.arange(TOK_G, dtype=jnp.int32)
    allowed = (position[None, :] <= position[:, None]) & (document[None, :] == document[:, None])
    masked = out_grad * response[:, None]
    kv_of_head = kv_order[jnp.arange(HQ, dtype=jnp.int32) // (HQ // KV)].astype(jnp.int32)
    query_heads = queries.reshape(TOK_G, HQ, HD).transpose(1, 0, 2)
    grad_heads = masked.reshape(TOK_G, HQ, HD).transpose(1, 0, 2)
    key_heads = jnp.take(keys.reshape(TOK_G, KV, HD).transpose(1, 0, 2), kv_of_head, axis=0)
    value_heads = jnp.take(values.reshape(TOK_G, KV, HD).transpose(1, 0, 2), kv_of_head, axis=0)

    def one_head(operands):
        query_rows, key_rows, value_rows, grad_rows = operands
        raw_scores = jnp.dot(query_rows, key_rows.T, preferred_element_type=jnp.float32) * scale_factor
        raw_scores = jnp.where(allowed, raw_scores, -jnp.inf)
        row_top = lax.optimization_barrier(jnp.max(raw_scores, axis=1, keepdims=True))
        exp_scores = jnp.exp(raw_scores - row_top)
        attention = exp_scores / lax.optimization_barrier(jnp.sum(exp_scores, axis=1, keepdims=True))
        attention_half = attention.astype(jnp.bfloat16)
        grad_value = jnp.dot(attention_half.T, grad_rows, preferred_element_type=jnp.float32)
        grad_attention = jnp.dot(grad_rows, value_rows.T, preferred_element_type=jnp.float32)
        row_delta = lax.optimization_barrier(jnp.sum(attention * grad_attention, axis=1, keepdims=True))
        grad_scores = (attention * (grad_attention - row_delta) * scale_factor).astype(jnp.bfloat16)
        grad_query = jnp.dot(grad_scores, key_rows, preferred_element_type=jnp.float32).astype(jnp.bfloat16)
        grad_key = jnp.dot(grad_scores.T, query_rows, preferred_element_type=jnp.float32)
        return (grad_query, grad_key, grad_value)
    head_query, head_key, head_value = lax.map(one_head, (query_heads, key_heads, value_heads, grad_heads))
    query_grad = head_query.transpose(1, 0, 2).reshape(TOK_G, HQ * HD)
    key_list = []
    value_list = []
    for kv_index in range(KV):
        chosen = (kv_of_head == kv_index)[:, None, None]
        key_list.append(lax.optimization_barrier(jnp.sum(jnp.where(chosen, head_key, jnp.zeros_like(head_key)), axis=0)))
        value_list.append(lax.optimization_barrier(jnp.sum(jnp.where(chosen, head_value, jnp.zeros_like(head_value)), axis=0)))
    key_grad = jnp.stack(key_list, axis=1).reshape(TOK_G, KV * HD)
    value_grad = jnp.stack(value_list, axis=1).reshape(TOK_G, KV * HD)
    return (query_grad, key_grad, value_grad)

def reference(queries, keys, values, out_grad, hidden_in, q_weight, lengths, kv_order):
    key_parts = []
    value_parts = []
    input_parts = []
    weight_grad = jnp.zeros((HQ * HD, D), jnp.float32)
    for rollout_group in range(N_ROLLOUT):
        row_first = rollout_group * TOK_G
        row_last = row_first + TOK_G
        query_grad, key_grad, value_grad = group_grads(queries[row_first:row_last], keys[row_first:row_last], values[row_first:row_last], out_grad[row_first:row_last], lengths[rollout_group], kv_order)
        key_parts.append(key_grad)
        value_parts.append(value_grad)
        input_parts.append(jnp.dot(query_grad, q_weight, preferred_element_type=jnp.float32).astype(jnp.bfloat16))
        weight_grad = weight_grad + jnp.dot(query_grad.T, hidden_in[row_first:row_last], preferred_element_type=jnp.float32)
    return (jnp.concatenate(key_parts, axis=0), jnp.concatenate(value_parts, axis=0), jnp.concatenate(input_parts, axis=0), weight_grad)
```

```python
import functools
import math

import jax
import jax.numpy as jnp
from jax import lax
from jax.experimental import pallas as pl
from jax.experimental.pallas import tpu as pltpu
from jax.sharding import PartitionSpec as P

HQ = 32
KV = 4
HD = 128
ROLLS = 16
BQ = 128


def pack_kernel(nrow, ncol, width, order_ref, q_ref, k_ref, v_ref, g_ref, out_ref):
    for r in range(nrow):
        for c in range(ncol):
            j = r * ncol + c
            first = (c * nrow + r) * width
            out_ref[j, :, 0:width] = q_ref[:, first : first + width]
            out_ref[j, :, width : 2 * width] = g_ref[:, first : first + width]
            kv = order_ref[first * KV // (HQ * HD)]
            columns = pl.ds(pl.multiple_of(kv * HD, HD), HD)
            out_ref[j, :, 2 * width : 2 * width + HD] = k_ref[:, columns]
            out_ref[j, :, 2 * width + HD : 2 * width + 2 * HD] = v_ref[:, columns]


def attend_kernel(reach, heads, start_ref, resp_ref, q_ref, g_ref, k_ref, v_ref, dq_ref, dkv_ref, acc):
    head = pl.program_id(0)
    length = q_ref.shape[0]
    scale = 1.0 / math.sqrt(HD)

    @pl.when(head == 0)
    def _():
        acc[...] = jnp.zeros_like(acc)

    for first in range(0, length, BQ):
        last = first + BQ
        low = max(0, first - reach)
        q = q_ref[first:last, :]
        resp = resp_ref[first:last, :]
        g = jnp.where(resp > 0, g_ref[first:last, :].astype(jnp.float32), 0.0).astype(jnp.bfloat16)
        k = k_ref[low:last, :]
        v = v_ref[low:last, :]
        shape = (BQ, last - low)
        col = low + lax.broadcasted_iota(jnp.int32, shape, 1)
        row = first + lax.broadcasted_iota(jnp.int32, shape, 0)
        allowed = (col <= row) & (col >= start_ref[first:last, :])
        s = lax.dot_general(q, k, (((1,), (1,)), ((), ())), preferred_element_type=jnp.float32)
        s = jnp.where(allowed, s * scale, -jnp.inf)
        e = jnp.exp(s - jnp.max(s, axis=1, keepdims=True))
        p = e * (1.0 / jnp.sum(e, axis=1, keepdims=True))
        dp = lax.dot_general(g, v, (((1,), (1,)), ((), ())), preferred_element_type=jnp.float32)
        delta = jnp.sum(p * dp, axis=1, keepdims=True)
        ds = (p * (dp - delta) * scale).astype(jnp.bfloat16)
        dq_ref[first:last, :] = jnp.dot(ds, k, preferred_element_type=jnp.float32).astype(jnp.bfloat16)
        acc[low:last, 0:HD] += lax.dot_general(
            ds, q, (((0,), (0,)), ((), ())), preferred_element_type=jnp.float32
        )
        acc[low:last, HD : 2 * HD] += lax.dot_general(
            p.astype(jnp.bfloat16), g, (((0,), (0,)), ((), ())), preferred_element_type=jnp.float32
        )

    @pl.when(head == heads - 1)
    def _():
        dkv_ref[...] = acc[...].astype(jnp.bfloat16)


def shift(x, axis, step):
    n = lax.axis_size(axis)
    return lax.ppermute(x, axis, [(i, (i + step) % n) for i in range(n)])


def flip(x, axis, bit):
    n = lax.axis_size(axis)
    return lax.ppermute(x, axis, [(i, i ^ bit) for i in range(n)])


def pick(stacked, index):
    return lax.dynamic_index_in_dim(stacked, index, 0, keepdims=False)


def dot32(a, b):
    return jnp.dot(a, b, preferred_element_type=jnp.float32)


def tdot32(a, b):
    return lax.dot_general(a, b, (((0,), (0,)), ((), ())), preferred_element_type=jnp.float32)


def gather_ring(x, axis):
    n = lax.axis_size(axis)
    me = lax.axis_index(axis)
    pieces = {0: x}
    if n == 4:
        half = x.shape[0] // 2
        pieces[1] = shift(x, axis, 1)
        pieces[3] = shift(x, axis, -1)
        pieces[2] = jnp.concatenate(
            [shift(pieces[1][:half], axis, 1), shift(pieces[3][half:], axis, -1)], axis=0
        )
    else:
        for s in range(1, n):
            pieces[s] = shift(x, axis, s)
    out = jnp.zeros((n,) + x.shape, x.dtype)
    for s in range(n):
        out = lax.dynamic_update_index_in_dim(out, pieces[s], (me - s) % n, 0)
    return out.reshape((n * x.shape[0],) + x.shape[1:])


def body(queries, keys, values, out_grad, hidden_in, q_weight, lengths, kv_order):
    nrow = lax.axis_size("row")
    ncol = lax.axis_size("col")
    nroll = lax.axis_size("rollout")
    row, col, roll = lax.axis_index("row"), lax.axis_index("col"), lax.axis_index("rollout")
    group = nrow * ncol
    token_dev = queries.shape[0]
    length = token_dev * group
    heads = HQ // group
    width = heads * HD
    reach = 2 * (length // ROLLS)
    reach = -(-reach // BQ) * BQ

    packed = pl.pallas_call(
        functools.partial(pack_kernel, nrow, ncol, width),
        out_shape=jax.ShapeDtypeStruct((group, token_dev, 2 * width + 2 * HD), jnp.bfloat16),
        in_specs=[pl.BlockSpec(memory_space=pltpu.SMEM)] + [pl.BlockSpec(memory_space=pltpu.VMEM)] * 4,
        out_specs=pl.BlockSpec(memory_space=pltpu.VMEM),
    )(kv_order, queries, keys, values, out_grad)
    got = lax.all_to_all(packed, ("row", "col"), split_axis=0, concat_axis=0, tiled=True)
    got = got.reshape(length, 2 * width + 2 * HD)

    hidden = gather_ring(hidden_in, "col")

    bounds = jnp.cumsum(lengths[0])
    position = jnp.arange(length, dtype=jnp.int32)
    reached = position[:, None] >= bounds[None, :]
    parts = jnp.sum(reached.astype(jnp.int32), axis=1, keepdims=True)
    resp = parts % 2
    start = jnp.max(
        jnp.where(reached[:, 1::2], bounds[None, 1::2], 0), axis=1, keepdims=True
    ).astype(jnp.int32)

    whole = lambda shape: pl.BlockSpec(shape, lambda h: (0, 0))
    block = (length, HD)
    pairs = length * (reach + BQ) * heads
    dq, dkv = pl.pallas_call(
        functools.partial(attend_kernel, reach, heads),
        grid=(heads,),
        out_shape=(
            jax.ShapeDtypeStruct((length, width), jnp.bfloat16),
            jax.ShapeDtypeStruct((length, 2 * HD), jnp.bfloat16),
        ),
        in_specs=[
            whole((length, 1)),
            whole((length, 1)),
            pl.BlockSpec(block, lambda h: (0, h)),
            pl.BlockSpec(block, lambda h: (0, heads + h)),
            pl.BlockSpec(block, lambda h: (0, 2 * heads)),
            pl.BlockSpec(block, lambda h: (0, 2 * heads + 1)),
        ],
        out_specs=(pl.BlockSpec(block, lambda h: (0, h)), whole((length, 2 * HD))),
        scratch_shapes=[pltpu.VMEM((length, 2 * HD), jnp.float32)],
        cost_estimate=pl.CostEstimate(
            flops=10 * pairs * HD, bytes_accessed=8 * length * width, transcendentals=pairs
        ),
    )(start, resp, got, got, got, got)

    near = jnp.stack([dq] + [shift(dq, "row", s) for s in range(1, nrow)])
    dq_col = jnp.concatenate([pick(near, (row - j) % nrow) for j in range(nrow)], axis=1)

    feats = dq_col.shape[1] // ncol
    by_col = dq_col.reshape(length, ncol, feats).transpose(1, 0, 2)
    got_feats = [pick(by_col, col)] + [
        shift(pick(by_col, (col + s) % ncol), "col", s) for s in range(1, ncol)
    ]
    stack = jnp.stack(got_feats)
    lane = [pick(stack, (col - (roll ^ k)) % ncol) for k in range(nroll)]

    by_tok = dq_col.reshape(ncol, length // ncol, dq_col.shape[1])
    part = lambda k: dot32(pick(by_tok, (col + k) % ncol), q_weight)
    low = jnp.bfloat16
    if ncol == 4:
        half = q_weight.shape[1] // 2
        far = part(2).astype(low)
        up = shift(far[:, :half], "col", 1)
        down = shift(far[:, half:], "col", -1)
        right, left = part(1), part(3)
        right = jnp.concatenate([right[:, :half] + up.astype(jnp.float32), right[:, half:]], axis=1)
        left = jnp.concatenate([left[:, :half], left[:, half:] + down.astype(jnp.float32)], axis=1)
        come = [shift(right.astype(low), "col", 1), shift(left.astype(low), "col", -1)]
    else:
        come = [shift(part(s).astype(low), "col", s) for s in range(1, ncol)]
    total = part(0)
    for piece in come:
        total = total + piece.astype(jnp.float32)
    input_grad = total.astype(low)

    alive = list(range(nroll))
    landed = {k: [] for k in alive}
    bit = 1
    while bit < nroll:
        go = [k for k in alive if k & bit]
        alive = [k for k in alive if not k & bit]
        for k in reversed(go):
            value = tdot32(lane[k], hidden)
            for piece in landed[k]:
                value = value + piece.astype(jnp.float32)
            landed[k ^ bit].append(flip(value.astype(low), "rollout", bit))
        bit *= 2
    weight_grad = tdot32(lane[0], hidden)
    for piece in landed[0]:
        weight_grad = weight_grad + piece.astype(jnp.float32)

    back = lax.all_to_all(
        dkv.reshape(group, token_dev, 2 * HD), ("row", "col"), split_axis=0, concat_axis=0, tiled=True
    )
    back = back.reshape(nrow, ncol, token_dev, 2 * HD).transpose(1, 0, 2, 3).astype(jnp.float32)
    summed = jnp.sum(back.reshape(KV, group // KV, token_dev, 2 * HD), axis=1)
    placed = [
        sum(jnp.where(kv_order[m] == k, summed[m], 0.0) for m in range(KV)) for k in range(KV)
    ]
    key_grad = jnp.concatenate([x[:, :HD] for x in placed], axis=1)
    value_grad = jnp.concatenate([x[:, HD:] for x in placed], axis=1)
    return (key_grad, value_grad, input_grad, weight_grad)


def solution(mesh):
    placed = (
        P(("rollout", "row", "col"), None),
        P(("rollout", "row", "col"), None),
        P(("rollout", "row", "col"), None),
        P(("rollout", "row", "col"), None),
        P(("rollout", "col"), "row"),
        P("col", "row"),
        P("rollout", None),
        P(),
    )
    return jax.shard_map(
        body,
        mesh=mesh,
        in_specs=placed,
        out_specs=(
            P(("rollout", "row", "col"), None),
            P(("rollout", "row", "col"), None),
            P(("rollout", "col"), "row"),
            P(("rollout", "col"), "row"),
        ),
        check_vma=False,
    )
```
